32 devices in a mesh: rows: 4 (over y, core), cols: 8 (over z, x).
Axes of the slice: x: 2, y: 2, z: 4, core: 2. Of those that a mesh axis runs over, the one named last changes fastest.
Arguments:
- costs: bfloat16 [4, 8, 24, 256, 256], P('rows', 'cols'), may hold values from -210 to 8
- block_rows: int32 [4, 8, 24], P('rows', 'cols'), may hold values from 0 to 7, as said below
- block_cols: int32 [4, 8, 24], P('rows', 'cols'), may hold values from 0 to 63, as said below
- live: int32 [4, 8], P('rows', 'cols'), may hold values from 16 to 24, as said below
- log_source: float32 [8192], P('rows'), may hold values from -6 to 6
- log_target: float32 [131072], P('cols'), may hold values from -6 to 6
Outputs:
- source_potential: float32 [8192], P('rows')
- target_potential: float32 [131072], P('cols')
The draws below stay inside these ranges and needn't reach their ends.
Inputs may be any that keep to these rules, and one draw needn't show every extreme that they name: `block_rows`: row blocks are local to a device's 8 blocks of source cells. `block_cols`: column blocks are local to a device's 64 blocks of target cells. Every source cell and every target cell lies in some live block. `live`: live counts differ from device to device; some device uses all 24 slots.
All inputs are finite; a program needn't handle non-finite values.
Results may differ from the reference program's by a relative error of at most 0.0003.
Values sent between devices are 32-bit elements; how exact they have to be, the bound alone decides.
A program may use at most 64 MiB of HBM per device.

```python
import jax
import jax.numpy as jnp
from jax import lax

BS = 256
RB_DEV = 8
CB_DEV = 64
EXTRA = 8
ITERS = 3
SLOTS = 24
SRC = 8192
TGT = 131072
N_ROWS = 4
N_COLS = 8


def pair_tables(key):
    base = jax.random.fold_in(key, 7)
    k_rows, k_band, k_live, k_busy = jax.random.split(base, 4)
    must = max(RB_DEV, CB_DEV // N_ROWS)
    share = CB_DEV // N_ROWS
    shape = (N_ROWS, N_COLS, SLOTS)
    slot_ids = jnp.broadcast_to(jnp.arange(SLOTS, dtype=jnp.int32)[None, None, :], shape)
    row_ids = jnp.broadcast_to(jnp.arange(N_ROWS, dtype=jnp.int32)[:, None, None], shape)
    extra_rows = jax.random.randint(k_rows, shape, 0, RB_DEV)
    extra_cols = extra_rows * CB_DEV // RB_DEV + jax.random.randint(k_band, shape, -4, 5)
    extra_cols = jnp.mod(extra_cols, CB_DEV)
    must_rows = jnp.mod(slot_ids, RB_DEV)
    must_cols = jnp.mod(slot_ids, share) * N_ROWS + row_ids
    rows_out = jnp.where(slot_ids < must, must_rows, extra_rows).astype(jnp.int32)
    cols_out = jnp.where(slot_ids < must, must_cols, extra_cols).astype(jnp.int32)
    extra_live = jax.random.randint(k_live, (N_ROWS * N_COLS,), 0, EXTRA + 1)
    busiest = jax.random.randint(k_busy, (), 0, N_ROWS * N_COLS)
    extra_live = jnp.where(jnp.arange(N_ROWS * N_COLS) == busiest, EXTRA, extra_live)
    live_out = (must + extra_live).reshape(N_ROWS, N_COLS).astype(jnp.int32)
    return (rows_out, cols_out, live_out)


def draw_block_rows(key, part):
    return pair_tables(key)[0]


def draw_block_cols(key, part):
    return pair_tables(key)[1]


def draw_live(key, part):
    return pair_tables(key)[2]


def draw_costs(key, part):
    shape = (N_ROWS, N_COLS, SLOTS, BS, BS)
    k_one = jax.random.fold_in(jax.random.fold_in(key, 11), 0)
    values = jnp.clip(2.0 * jax.random.normal(k_one, shape, jnp.float32), -8.0, 8.0)
    return values.astype(jnp.bfloat16)


def shard_levels(stream_key, extent, shards, low, largest):
    factor_of = 1.0
    for dim, shards_of in shards:
        heights = jax.random.uniform(jax.random.fold_in(jax.random.fold_in(stream_key, 6), dim), (shards_of,), jnp.float32, low / len(shards), largest / len(shards))
        factor_of = factor_of * jnp.repeat(jnp.exp(heights), extent[dim] // shards_of).reshape((-1,) + (1,) * (len(extent) - 1 - dim))
    return factor_of


def centred(stream_key, shape, width, reach, cuts=(), kind=jnp.bfloat16):
    loudness = shard_levels(stream_key, shape, cuts, -0.22, 0.18) if cuts else 1.0
    values = jax.random.normal(stream_key, shape, jnp.float32) * width * loudness
    return jnp.minimum(jnp.maximum(values, -reach), reach).astype(kind)


def setup_inputs(seed: int = 0) -> dict:
    key_list = jax.random.split(jax.random.key(seed), 7)
    return {
        "costs": draw_costs(jax.random.fold_in(key_list[6], 71), 0),
        "block_rows": draw_block_rows(jax.random.fold_in(key_list[6], 71), 0),
        "block_cols": draw_block_cols(jax.random.fold_in(key_list[6], 71), 0),
        "live": draw_live(jax.random.fold_in(key_list[6], 71), 0),
        "log_source": centred(key_list[4], (SRC,), 1.0, 6.0, ((0, 4),), jnp.float32),
        "log_target": centred(key_list[5], (TGT,), 1.0, 6.0, ((0, 8),), jnp.float32),
    }


NEG = -1e30


def reference(costs, block_rows, block_cols, live, log_source, log_target):
    nr, nc, slots, bs, _ = costs.shape
    tiles = costs.reshape(nr * nc * slots, bs, bs)
    dev_r = jnp.broadcast_to(jnp.arange(nr, dtype=jnp.int32)[:, None, None], (nr, nc, slots)).reshape(-1)
    dev_c = jnp.broadcast_to(jnp.arange(nc, dtype=jnp.int32)[None, :, None], (nr, nc, slots)).reshape(-1)
    slot_ids = jnp.broadcast_to(jnp.arange(slots, dtype=jnp.int32)[None, None, :], (nr, nc, slots))
    valid = (slot_ids < live[:, :, None]).reshape(-1)
    row_start = ((dev_r * RB_DEV + block_rows.reshape(-1)) * bs).astype(jnp.int32)
    col_start = ((dev_c * CB_DEV + block_cols.reshape(-1)) * bs).astype(jnp.int32)
    items = (tiles, row_start, col_start, valid)

    def row_lse(target_pot):
        def step(carry, item):
            top, total = carry
            tile, rs, cs, okay = item
            score = lax.dynamic_slice_in_dim(target_pot, cs, bs)[None, :] - tile.astype(jnp.float32)
            old_top = lax.dynamic_slice_in_dim(top, rs, bs)
            old_tot = lax.dynamic_slice_in_dim(total, rs, bs)
            new_top = jnp.maximum(old_top, jnp.max(score, axis=1))
            new_tot = old_tot * jnp.exp(old_top - new_top) + jnp.sum(jnp.exp(score - new_top[:, None]), axis=1)
            new_top = jnp.where(okay, new_top, old_top)
            new_tot = jnp.where(okay, new_tot, old_tot)
            top = lax.dynamic_update_slice_in_dim(top, new_top, rs, 0)
            total = lax.dynamic_update_slice_in_dim(total, new_tot, rs, 0)
            return (top, total), None
        init = (jnp.full((SRC,), NEG, jnp.float32), jnp.zeros((SRC,), jnp.float32))
        (top, total), _ = lax.scan(step, init, items)
        return top + jnp.log(total)

    def col_lse(source_pot):
        def step(carry, item):
            top, total = carry
            tile, rs, cs, okay = item
            score = lax.dynamic_slice_in_dim(source_pot, rs, bs)[:, None] - tile.astype(jnp.float32)
            old_top = lax.dynamic_slice_in_dim(top, cs, bs)
            old_tot = lax.dynamic_slice_in_dim(total, cs, bs)
            new_top = jnp.maximum(old_top, jnp.max(score, axis=0))
            new_tot = old_tot * jnp.exp(old_top - new_top) + jnp.sum(jnp.exp(score - new_top[None, :]), axis=0)
            new_top = jnp.where(okay, new_top, old_top)
            new_tot = jnp.where(okay, new_tot, old_tot)
            top = lax.dynamic_update_slice_in_dim(top, new_top, cs, 0)
            total = lax.dynamic_update_slice_in_dim(total, new_tot, cs, 0)
            return (top, total), None
        init = (jnp.full((TGT,), NEG, jnp.float32), jnp.zeros((TGT,), jnp.float32))
        (top, total), _ = lax.scan(step, init, items)
        return top + jnp.log(total)

    target_pot = jnp.zeros((TGT,), jnp.float32)
    source_pot = jnp.zeros((SRC,), jnp.float32)
    for sweep in range(ITERS):
        source_pot = log_source - row_lse(target_pot)
        target_pot = log_target - col_lse(source_pot)
    return source_pot, target_pot
```

```python
import functools

import jax
import jax.numpy as jnp
from jax import lax
from jax.experimental import pallas as pl
from jax.experimental.pallas import tpu as pltpu
from jax.sharding import PartitionSpec as P

ITERS = 3
NEG = -1e30
LOG2E = 1.4426950408889634
LN2 = 0.6931471805599453
LANES = 128
GROUP = 8
HEAD = 28.0
SCALE = 66.0
MESH = pl.DeviceIdType.MESH


def log2(x):
    return jnp.log(x) * LOG2E


def split_peer(me, k, n):
    if n & (n - 1):
        return lax.rem(me + k, n), lax.rem(me + n - k, n)
    other = me
    bit = 1
    while bit <= k:
        if k & bit:
            other = other + bit - 2 * bit * lax.rem(lax.div(me, bit), 2)
        bit *= 2
    return other, other


def kernel(
    n_rows, n_cols,
    brows, bcols, live, costs, log_src, log_tgt,
    src_out, lse_out, ids_out,
    tiles, tiles_s, tiles_t, rid, cid, base, slot_tot, part_src, part_tgt, src_row, columns, weight, lt_piece,
    cid_all, src_buf, tgt_buf,
    load_sem, cid_send, cid_recv, src_send, src_recv, tgt_send, tgt_recv,
):
    slots, bs, _ = tiles.shape
    halves = bs // LANES
    row_blocks = src_row.shape[0]
    my_r = lax.axis_index("rows")
    my_c = lax.axis_index("cols")

    barrier = pltpu.get_barrier_semaphore()
    for k in range(n_cols - 1, 0, -1):
        pl.semaphore_signal(barrier, inc=1, device_id=(my_r, split_peer(my_c, k, n_cols)[0]), device_id_type=MESH)
    for k in range(n_rows - 1, 0, -1):
        pl.semaphore_signal(barrier, inc=1, device_id=(split_peer(my_r, k, n_rows)[0], my_c), device_id_type=MESH)

    loads = []
    for c in range(slots // GROUP):
        part = pl.ds(c * GROUP, GROUP)
        loads.append(pltpu.make_async_copy(costs.at[part], tiles.at[part], load_sem.at[c]))
        loads[-1].start()

    count = live[0]
    for t in range(slots):
        okay = t < count
        rid[t : t + 1, :] = jnp.full((1, bs), jnp.where(okay, brows[t], -1), jnp.int32)
        cid[t : t + 1, :] = jnp.full((1, bs), jnp.where(okay, bcols[t], -1), jnp.int32)
    cid_all[pl.ds(my_r, 1)] = cid[:, :LANES][None]

    def exchange(along, n, me, src, buf, send_sem, recv_sem):
        copies = []
        for k in range(n - 1, 0, -1):
            to = split_peer(me, k, n)[0]
            peer = (to, my_c) if along == "rows" else (my_r, to)
            copies.append(pltpu.make_async_remote_copy(
                src_ref=src, dst_ref=buf.at[me], send_sem=send_sem.at[k], recv_sem=recv_sem.at[k],
                device_id=peer, device_id_type=MESH))
            copies[-1].start()
        return copies

    def arrived(along, n, me, src, buf, send_sem, recv_sem):
        for k in range(1, n):
            to, frm = split_peer(me, k, n)
            peer = (to, my_c) if along == "rows" else (my_r, to)
            pltpu.make_async_remote_copy(
                src_ref=src, dst_ref=buf.at[frm], send_sem=send_sem.at[k], recv_sem=recv_sem.at[k],
                device_id=peer, device_id_type=MESH).wait_recv()

    def as_column(row):
        return jnp.concatenate(
            [jnp.broadcast_to(row[:, h * LANES : (h + 1) * LANES], (LANES, LANES)).T for h in range(halves)], axis=0)

    def groups(body):
        def step(g, _):
            body(g, pl.ds(pl.multiple_of(g * GROUP, GROUP), GROUP))
            return 0

        lax.fori_loop(0, slots // GROUP, step, 0)

    cuts = [slice(h * LANES, (h + 1) * LANES) for h in range(halves)]
    eye = (lax.broadcasted_iota(jnp.int32, (bs, bs), 0) == lax.broadcasted_iota(jnp.int32, (bs, bs), 1))
    eye = eye.astype(jnp.float32).astype(jnp.bfloat16)
    for c in range(slots // GROUP):
        loads[c].wait()

        def turn(t, _):
            tile = tiles[t]
            turned = lax.dot_general(eye, tile, (((1,), (1,)), ((), ())), preferred_element_type=jnp.float32)
            tiles_t[t] = turned * LOG2E
            tiles_s[t] = tile.astype(jnp.float32) * LOG2E
            return 0

        lax.fori_loop(c * GROUP, (c + 1) * GROUP, turn, 0, unroll=2)
        at = slice(c * GROUP, (c + 1) * GROUP)
        for lanes in cuts:
            lows, tots = [], []
            for i in range(GROUP):
                cost = tiles_t[c * GROUP + i, :, lanes]
                low = jnp.min(cost, axis=0, keepdims=True)
                lows.append(low)
                tots.append(jnp.sum(jnp.exp2(low - cost), axis=0, keepdims=True))
            base[at, lanes] = -jnp.concatenate(lows, axis=0)
            slot_tot[at, lanes] = jnp.concatenate(tots, axis=0)

    block_of = lax.broadcasted_iota(jnp.int32, (row_blocks, bs), 0)
    found = base[...] + log2(slot_tot[...])
    masked = [jnp.where(block_of == rid[t : t + 1, :], found[t : t + 1, :], NEG) for t in range(slots)]
    top = functools.reduce(jnp.maximum, masked)
    total = functools.reduce(jnp.add, [jnp.exp2(value - top) for value in masked])
    part_src[0] = top + log2(total)
    src_buf[0, pl.ds(my_c, 1)] = part_src[0][None]

    pl.semaphore_wait(barrier, n_rows + n_cols - 2)

    def send_src(sweep):
        return exchange("cols", n_cols, my_c, part_src.at[sweep], src_buf.at[sweep], src_send.at[sweep], src_recv.at[sweep])

    def get_src(sweep):
        arrived("cols", n_cols, my_c, part_src.at[sweep], src_buf.at[sweep], src_send.at[sweep], src_recv.at[sweep])
        return [src_buf[sweep, k] for k in range(n_cols)]

    def send_tgt(sweep):
        return exchange("rows", n_rows, my_r, part_tgt.at[sweep], tgt_buf.at[sweep], tgt_send.at[sweep], tgt_recv.at[sweep])

    def get_tgt(sweep):
        arrived("rows", n_rows, my_r, part_tgt.at[sweep], tgt_buf.at[sweep], tgt_send.at[sweep], tgt_recv.at[sweep])

    waits = send_src(0)
    waits += exchange("rows", n_rows, my_r, cid_all.at[my_r], cid_all, cid_send, cid_recv)

    for t in range(slots):
        col_at = bcols[t] * halves
        for h, lanes in enumerate(cuts):
            lt_piece[t : t + 1, lanes] = log_tgt[pl.ds(col_at + h, 1), :] * LOG2E
    log_a = jnp.concatenate([log_src[pl.ds(h, row_blocks, stride=halves), :] for h in range(halves)], axis=1) * LOG2E

    theirs = get_src(0)
    top = functools.reduce(jnp.maximum, theirs)
    total = functools.reduce(jnp.add, [jnp.exp2(value - top) for value in theirs])
    first = log_a - (top + log2(total))
    src_row[...] = first

    def put_columns(values):
        for b in range(row_blocks):
            columns[b] = as_column(values[b : b + 1, :])

    put_columns(first)

    def first_col(g, at):
        for lanes in cuts:
            tops, tots = [], []
            for i in range(GROUP):
                t = g * GROUP + i
                score = columns[brows[t]] - tiles_s[t, :, lanes]
                top = jnp.max(score, axis=0, keepdims=True) - HEAD
                entry = jnp.exp2(score - top)
                tiles_s[t, :, lanes] = entry
                tops.append(top)
                tots.append(jnp.sum(entry, axis=0, keepdims=True))
            base[at, lanes] = jnp.concatenate(tops, axis=0)
            slot_tot[at, lanes] = jnp.concatenate(tots, axis=0)

    groups(first_col)
    alive = cid[...] >= 0
    part_tgt[0] = jnp.where(alive, base[...] + log2(slot_tot[...]), NEG)
    tgt_buf[0, pl.ds(my_r, 1)] = part_tgt[0][None]
    waits += send_tgt(0)

    def first_turned(g, at):
        bases = base[at, :]
        for i in range(GROUP):
            t = g * GROUP + i
            down = as_column(bases[i : i + 1])
            row = src_row[pl.ds(brows[t], 1), :]
            for lanes in cuts:
                tiles_t[t, :, lanes] = jnp.exp2((row[:, lanes] - tiles_t[t, :, lanes]) - down)

    groups(first_turned)
    arrived("rows", n_rows, my_r, cid_all.at[my_r], cid_all, cid_send, cid_recv)
    get_tgt(0)

    def candidates(sweep, lanes, fill):
        ids = cid[:, :LANES]

        def each(g):
            at = pl.ds(pl.multiple_of(g * GROUP, GROUP), GROUP)
            for r in range(n_rows):
                theirs, values = cid_all[r, at, :], tgt_buf[sweep, r, at, lanes]
                for i in range(GROUP):
                    yield jnp.where(ids == theirs[i : i + 1], values[i : i + 1], fill)

        def fold(op, start):
            return lax.fori_loop(0, slots // GROUP, lambda g, so_far: functools.reduce(op, each(g), so_far), start)

        return fold

    for lanes in cuts:
        fold = candidates(0, lanes, NEG)
        top = fold(jnp.maximum, jnp.full((slots, LANES), NEG, jnp.float32))
        total = fold(lambda so_far, value: so_far + jnp.exp2(value - top), jnp.zeros((slots, LANES), jnp.float32))
        gain = lt_piece[:, lanes] - (top + log2(total)) + (base[:, lanes] + SCALE)
        weight[:, lanes] = jnp.where(cid[:, lanes] >= 0, jnp.exp2(gain), 0.0)
    anchor = weight[...]
    goal_a = jnp.exp2(log_a + SCALE)

    for sweep in range(1, ITERS):
        def row_sums(g, at):
            rows = weight[at, :]
            sums = []
            for i in range(GROUP):
                t = g * GROUP + i
                down = as_column(rows[i : i + 1])
                sums.append(jnp.concatenate(
                    [jnp.sum(tiles_t[t, :, lanes] * down, axis=0, keepdims=True) for lanes in cuts], axis=1))
            slot_tot[at, :] = jnp.concatenate(sums, axis=0)

        groups(row_sums)
        part_src[sweep] = functools.reduce(
            jnp.add, [jnp.where(block_of == rid[t : t + 1, :], slot_tot[t : t + 1, :], 0.0) for t in range(slots)])
        src_buf[sweep, pl.ds(my_c, 1)] = part_src[sweep][None]
        waits += send_src(sweep)
        scaling = goal_a / functools.reduce(jnp.add, get_src(sweep))
        put_columns(scaling)

        def col_sums(g, at):
            sums = []
            for i in range(GROUP):
                t = g * GROUP + i
                down = columns[brows[t]]
                sums.append(jnp.concatenate(
                    [jnp.sum(tiles_s[t, :, lanes] * down, axis=0, keepdims=True) for lanes in cuts], axis=1))
            slot_tot[at, :] = jnp.concatenate(sums, axis=0)

        groups(col_sums)
        if sweep < ITERS - 1:
            part_tgt[sweep] = anchor * slot_tot[...]
        else:
            part_tgt[sweep] = jnp.where(alive, base[...] + log2(slot_tot[...]), NEG)
        tgt_buf[sweep, pl.ds(my_r, 1)] = part_tgt[sweep][None]
        waits += send_tgt(sweep)
        if sweep < ITERS - 1:
            goal_b = jnp.exp2(lt_piece[...] + SCALE)
        else:
            src_out[...] = (src_row[...] + log2(scaling)) * LN2
        get_tgt(sweep)
        if sweep == ITERS - 1:
            for r in range(n_rows):
                lse_out[r * slots : (r + 1) * slots, :] = tgt_buf[sweep, r]
                ids_out[r * slots : (r + 1) * slots, :] = cid_all[r]
            continue
        for lanes in cuts:
            total = candidates(sweep, lanes, 0.0)(jnp.add, jnp.zeros((slots, LANES), jnp.float32))
            weight[:, lanes] = jnp.where(
                cid[:, lanes] >= 0, anchor[:, lanes] * (goal_b[:, lanes] / total), 0.0)
    for copy in waits:
        copy.wait_send()


def final_kernel(source, lse, ids, log_tgt, src_out, tgt_out, top_buf):
    found, bs = lse.shape
    halves = bs // LANES
    blocks = tgt_out.shape[0] // halves
    exact = functools.partial(jnp.dot, preferred_element_type=jnp.float32, precision=lax.Precision.HIGHEST)
    per = 16 if blocks % 16 == 0 else blocks
    for b in range(0, blocks, per):
        block = lax.broadcasted_iota(jnp.int32, (per, LANES), 0) + b

        def top_of(g, top):
            at = pl.ds(pl.multiple_of(g * GROUP, GROUP), GROUP)
            theirs, values = ids[at, :], lse[at, :]
            for i in range(GROUP):
                here = jnp.concatenate([block == theirs[i : i + 1]] * halves, axis=1)
                top = jnp.maximum(top, jnp.where(here, values[i : i + 1], NEG))
            return top

        top_buf[b : b + per, :] = lax.fori_loop(
            0, found // GROUP, top_of, jnp.full((per, bs), NEG, jnp.float32), unroll=3 if found % (3 * GROUP) == 0 else 2)
    top = top_buf[...]
    names = ids[...].astype(jnp.float32)
    back = (names[:, 0:1] == lax.broadcasted_iota(jnp.int32, (found, blocks), 1).astype(jnp.float32)).astype(jnp.float32)
    into = (names.T[0:1, :] == lax.broadcasted_iota(jnp.int32, (blocks, found), 0).astype(jnp.float32)).astype(jnp.float32)
    total = exact(into, jnp.exp2(lse[...] - exact(back, top)))
    found_lse = top * LN2 + jnp.log(total)
    for h in range(halves):
        rows = pl.ds(h, blocks, stride=halves)
        tgt_out[rows, :] = log_tgt[rows, :] - found_lse[:, h * LANES : (h + 1) * LANES]
        src_out[pl.ds(h, source.shape[0], stride=halves), :] = source[:, h * LANES : (h + 1) * LANES]


def per_device(n_rows, n_cols, costs, block_rows, block_cols, live, log_source, log_target):
    tiles = costs[0, 0]
    slots, bs, _ = tiles.shape
    src_rows = log_source.shape[0] // LANES
    tgt_rows = log_target.shape[0] // LANES
    row_blocks = log_source.shape[0] // bs
    f32 = jnp.float32
    halves = bs // LANES
    dma = pltpu.SemaphoreType.DMA
    smem = pl.BlockSpec(memory_space=pltpu.SMEM)
    vmem = pl.BlockSpec(memory_space=pltpu.VMEM)
    found = n_rows * slots
    source, lse, ids = pl.pallas_call(
        functools.partial(kernel, n_rows, n_cols),
        out_shape=(
            jax.ShapeDtypeStruct((row_blocks, bs), f32),
            jax.ShapeDtypeStruct((found, bs), f32),
            jax.ShapeDtypeStruct((found, LANES), jnp.int32),
        ),
        in_specs=[smem, smem, smem, pl.BlockSpec(memory_space=pl.ANY), vmem, vmem],
        out_specs=(vmem, vmem, vmem),
        scratch_shapes=[
            pltpu.VMEM((slots, bs, bs), tiles.dtype),
            pltpu.VMEM((slots, bs, bs), f32),
            pltpu.VMEM((slots, bs, bs), f32),
            pltpu.VMEM((slots, bs), jnp.int32),
            pltpu.VMEM((slots, bs), jnp.int32),
            pltpu.VMEM((slots, bs), f32),
            pltpu.VMEM((slots, bs), f32),
            pltpu.VMEM((ITERS, row_blocks, bs), f32),
            pltpu.VMEM((ITERS, slots, bs), f32),
            pltpu.VMEM((row_blocks, bs), f32),
            pltpu.VMEM((row_blocks, bs, LANES), f32),
            pltpu.VMEM((slots, bs), f32),
            pltpu.VMEM((slots, bs), f32),
            pltpu.VMEM((n_rows, slots, LANES), jnp.int32),
            pltpu.VMEM((ITERS, n_cols, row_blocks, bs), f32),
            pltpu.VMEM((ITERS, n_rows, slots, bs), f32),
            dma((slots // GROUP,)),
            dma((n_rows,)), dma((n_rows,)),
            dma((ITERS, n_cols)), dma((ITERS, n_cols)),
            dma((ITERS, n_rows)), dma((ITERS, n_rows)),
        ],
        compiler_params=pltpu.CompilerParams(collective_id=0, has_side_effects=True),
    )(
        block_rows.reshape(-1), block_cols.reshape(-1), live.reshape(-1), tiles,
        log_source.reshape(src_rows, LANES), log_target.reshape(tgt_rows, LANES),
    )
    source, target = pl.pallas_call(
        final_kernel,
        out_shape=(jax.ShapeDtypeStruct((src_rows, LANES), f32), jax.ShapeDtypeStruct((tgt_rows, LANES), f32)),
        in_specs=[vmem] * 4,
        out_specs=(vmem, vmem),
        scratch_shapes=[pltpu.VMEM((tgt_rows * LANES // bs, bs), f32)],
    )(source, lse, ids, log_target.reshape(tgt_rows, LANES))
    return source.reshape(-1), target.reshape(-1)


def solution(mesh):
    in_specs = (
        P("rows", "cols", None, None, None),
        P("rows", "cols", None),
        P("rows", "cols", None),
        P("rows", "cols"),
        P("rows"),
        P("cols"),
    )
    out_specs = (P("rows"), P("cols"))
    body = functools.partial(per_device, mesh.shape["rows"], mesh.shape["cols"])
    return jax.shard_map(body, mesh=mesh, in_specs=in_specs, out_specs=out_specs, check_vma=False)
```

```python
import functools

import jax
import jax.numpy as jnp
from jax import lax
from jax.experimental import pallas as pl
from jax.experimental.pallas import tpu as pltpu
from jax.sharding import PartitionSpec as P

ITERS = 3
NEG = -1e30
LOG2E = 1.4426950408889634
LN2 = 0.6931471805599453
LANES = 128
GROUP = 8
UNROLL = 1
HEAD = 28.0
SCALE = 66.0
MESH = pl.DeviceIdType.MESH


def log2(x):
    return jnp.log(x) * LOG2E


def split_peer(me, k, n):
    if n & (n - 1):
        return lax.rem(me + k, n), lax.rem(me + n - k, n)
    other = me
    bit = 1
    while bit <= k:
        if k & bit:
            other = other + bit - 2 * bit * lax.rem(lax.div(me, bit), 2)
        bit *= 2
    return other, other


def kernel(
    n_rows, n_cols,
    brows, bcols, live, costs, log_src, log_tgt,
    src_out, sums_out, into_out, offset_out,
    tiles, tiles_s, tiles_t, rid, cid, base, slot_tot, part_src, src_row, columns, anchor, weight, lt_piece, names, order,
    cid_all, src_buf, tgt_buf,
    load_sem, cid_send, cid_recv, src_send, src_recv, tgt_send, tgt_recv,
):
    slots, bs, _ = tiles.shape
    halves = bs // LANES
    row_blocks = src_row.shape[0]
    my_r = lax.axis_index("rows")
    my_c = lax.axis_index("cols")

    barrier = pltpu.get_barrier_semaphore()
    for k in range(n_cols - 1, 0, -1):
        pl.semaphore_signal(barrier, inc=1, device_id=(my_r, split_peer(my_c, k, n_cols)[0]), device_id_type=MESH)
    for k in range(n_rows - 1, 0, -1):
        pl.semaphore_signal(barrier, inc=1, device_id=(split_peer(my_r, k, n_rows)[0], my_c), device_id_type=MESH)

    loads = []
    for c in range(slots // GROUP):
        part = pl.ds(c * GROUP, GROUP)
        loads.append(pltpu.make_async_copy(costs.at[part], tiles.at[part], load_sem.at[c]))
        loads[-1].start()

    count = live[0]
    for t in range(slots):
        okay = t < count
        rid[t : t + 1, :] = jnp.full((1, bs), jnp.where(okay, brows[t], -1), jnp.int32)
        cid[t : t + 1, :] = jnp.full((1, bs), jnp.where(okay, bcols[t], -1), jnp.int32)
    cid_all[0] = cid[:, :LANES]

    def remote(along, k, src, dst, send_sem, recv_sem):
        if along == "rows":
            peer = (split_peer(my_r, k, n_rows)[0], my_c)
        else:
            peer = (my_r, split_peer(my_c, k, n_cols)[0])
        return pltpu.make_async_remote_copy(
            src_ref=src, dst_ref=dst, send_sem=send_sem.at[k], recv_sem=recv_sem.at[k],
            device_id=peer, device_id_type=MESH)

    def start(copies):
        for copy in copies:
            copy.start()
        return copies

    def as_column(row):
        return jnp.concatenate(
            [jnp.broadcast_to(row[:, h * LANES : (h + 1) * LANES], (LANES, LANES)).T for h in range(halves)], axis=0)

    def groups(body):
        def step(g, _):
            body(g, pl.ds(pl.multiple_of(g * GROUP, GROUP), GROUP))
            return 0

        lax.fori_loop(0, slots // GROUP, step, 0, unroll=UNROLL)

    cuts = [slice(h * LANES, (h + 1) * LANES) for h in range(halves)]
    eye = (lax.broadcasted_iota(jnp.int32, (bs, bs), 0) == lax.broadcasted_iota(jnp.int32, (bs, bs), 1))
    eye = eye.astype(jnp.float32).astype(jnp.bfloat16)
    for c in range(slots // GROUP):
        loads[c].wait()

        at = slice(c * GROUP, (c + 1) * GROUP)
        for lanes in cuts:
            lows, tots = [], []
            for t in range(c * GROUP, (c + 1) * GROUP):
                turned = lax.dot_general(
                    eye, tiles[t, lanes, :], (((1,), (1,)), ((), ())), preferred_element_type=jnp.float32)
                cost = turned * LOG2E
                tiles_t[t, :, lanes] = cost
                low = jnp.min(cost, axis=0, keepdims=True)
                lows.append(low)
                tots.append(jnp.sum(jnp.exp2(low - cost), axis=0, keepdims=True))
            base[at, lanes] = -jnp.concatenate(lows, axis=0)
            slot_tot[at, lanes] = jnp.concatenate(tots, axis=0)

    block_of = lax.broadcasted_iota(jnp.int32, (row_blocks, bs), 0)
    found = base[...] + log2(slot_tot[...])
    masked = [jnp.where(block_of == rid[t : t + 1, :], found[t : t + 1, :], NEG) for t in range(slots)]
    top = functools.reduce(jnp.maximum, masked)
    total = functools.reduce(jnp.add, [jnp.exp2(value - top) for value in masked])
    part_src[0] = top + log2(total)
    src_buf[0, pl.ds(my_c, 1)] = part_src[0][None]

    pl.semaphore_wait(barrier, n_rows + n_cols - 2)

    def send_src(sweep):
        return start([
            remote("cols", k, part_src.at[sweep], src_buf.at[sweep, my_c], src_send.at[sweep], src_recv.at[sweep])
            for k in range(n_cols - 1, 0, -1)])

    def get_src(sweep):
        for k in range(1, n_cols):
            frm = split_peer(my_c, k, n_cols)[1]
            remote("cols", k, part_src.at[sweep], src_buf.at[sweep, frm], src_send.at[sweep], src_recv.at[sweep]).wait_recv()
        return [src_buf[sweep, k] for k in range(n_cols)]

    def tgt_copy(sweep, k):
        return remote("rows", k, tgt_buf.at[sweep, 0], tgt_buf.at[sweep, k], tgt_send.at[sweep], tgt_recv.at[sweep])

    def send_tgt(sweep):
        return start([tgt_copy(sweep, k) for k in range(n_rows - 1, 0, -1)])

    def cid_copy(k):
        return remote("rows", k, cid_all.at[0], cid_all.at[k], cid_send, cid_recv)

    waits = send_src(0)
    waits += start([cid_copy(k) for k in range(n_rows - 1, 0, -1)])

    def natural(g, at):
        for i in range(GROUP):
            tiles_s[g * GROUP + i] = tiles[g * GROUP + i].astype(jnp.float32) * LOG2E

    groups(natural)

    for t in range(slots):
        col_at = bcols[t] * halves
        for h, lanes in enumerate(cuts):
            lt_piece[t : t + 1, lanes] = log_tgt[pl.ds(col_at + h, 1), :] * LOG2E
    log_a = jnp.concatenate([log_src[pl.ds(h, row_blocks, stride=halves), :] for h in range(halves)], axis=1) * LOG2E

    theirs = get_src(0)
    top = functools.reduce(jnp.maximum, theirs)
    total = functools.reduce(jnp.add, [jnp.exp2(value - top) for value in theirs])
    first = log_a - (top + log2(total))
    src_row[...] = first

    def put_columns(values):
        for b in range(row_blocks):
            columns[b] = as_column(values[b : b + 1, :])

    put_columns(first)

    def first_col(g, at):
        for lanes in cuts:
            tops, tots = [], []
            for i in range(GROUP):
                t = g * GROUP + i
                score = columns[brows[t]] - tiles_s[t, :, lanes]
                top = jnp.max(score, axis=0, keepdims=True) - HEAD
                entry = jnp.exp2(score - top)
                tiles_s[t, :, lanes] = entry
                tops.append(top)
                tots.append(jnp.sum(entry, axis=0, keepdims=True))
            base[at, lanes] = jnp.concatenate(tops, axis=0)
            slot_tot[at, lanes] = jnp.concatenate(tots, axis=0)

    groups(first_col)
    alive = cid[...] >= 0
    tgt_buf[0, 0] = jnp.where(alive, base[...] + log2(slot_tot[...]), NEG)
    waits += send_tgt(0)

    def first_turned(g, at):
        bases = base[at, :]
        for i in range(GROUP):
            t = g * GROUP + i
            down = as_column(bases[i : i + 1])
            row = src_row[pl.ds(brows[t], 1), :]
            for lanes in cuts:
                tiles_t[t, :, lanes] = jnp.exp2((row[:, lanes] - tiles_t[t, :, lanes]) - down)

    groups(first_turned)
    for k in range(1, n_rows):
        cid_copy(k).wait_recv()

    def wide(mask):
        return jnp.concatenate([mask] * halves, axis=1)

    def fold(sweep, k, op, so_far, fill):
        ids = cid[:, :LANES]

        def body(g, so_far):
            at = pl.ds(pl.multiple_of(g * GROUP, GROUP), GROUP)
            theirs, values = cid_all[k, at, :], tgt_buf[sweep, k, at, :]
            for i in range(GROUP):
                so_far = op(so_far, jnp.where(wide(ids == theirs[i : i + 1]), values[i : i + 1], fill))
            return so_far

        return lax.fori_loop(0, slots // GROUP, body, so_far, unroll=n_rows <= 4)

    top = jnp.full((slots, bs), NEG, jnp.float32)
    for k in range(n_rows):
        if k:
            tgt_copy(0, k).wait_recv()
        top = fold(0, k, jnp.maximum, top, NEG)
    total = jnp.zeros((slots, bs), jnp.float32)
    for k in range(n_rows):
        total = fold(0, k, lambda so_far, value: so_far + jnp.exp2(value - top), total, NEG)
    gain = lt_piece[...] - (top + log2(total)) + (base[...] + SCALE)
    anchor[...] = jnp.where(alive, jnp.exp2(gain), 0.0)
    weight[...] = anchor[...]
    goal_a = jnp.exp2(log_a + SCALE)

    def dense():
        blocks = offset_out.shape[0]
        padded = sums_out.shape[0]
        if padded > n_rows * slots:
            names[n_rows * slots :, :] = jnp.full((padded - n_rows * slots, LANES), -2.0, jnp.float32)
        for k in range(n_rows):
            frm = split_peer(my_r, k, n_rows)[1]
            names[pl.ds(pl.multiple_of(frm * slots, GROUP), slots), :] = cid_all[k].astype(jnp.float32)
            order[pl.ds(pl.multiple_of(frm * slots, GROUP), slots), :] = tgt_buf[0, k]
        for j in range(padded // LANES):
            line = names[j * LANES : (j + 1) * LANES, :].T[0:1, :]
            into_out[:, j * LANES : (j + 1) * LANES] = jnp.where(
                line == lax.broadcasted_iota(jnp.int32, (blocks, LANES), 0).astype(jnp.float32), 1.0, 0.0)
        per = 16 if blocks % 16 == 0 else blocks
        for b in range(0, blocks, per):
            block = (lax.broadcasted_iota(jnp.int32, (per, LANES), 0) + b).astype(jnp.float32)

            def walk(op, start):
                def body(g, so_far):
                    at = pl.ds(pl.multiple_of(g * GROUP, GROUP), GROUP)
                    theirs, values = names[at, :], order[at, :]
                    for i in range(GROUP):
                        so_far = op(so_far, jnp.where(wide(block == theirs[i : i + 1]), values[i : i + 1], NEG))
                    return so_far

                return lax.fori_loop(0, n_rows * slots // GROUP, body, start)

            top = walk(jnp.maximum, jnp.full((per, bs), NEG, jnp.float32))
            total = walk(lambda so_far, value: so_far + jnp.exp2(value - top), jnp.zeros((per, bs), jnp.float32))
            goal = jnp.concatenate(
                [log_tgt[pl.ds(b * halves + h, per, stride=halves), :] for h in range(halves)], axis=1) * LOG2E
            offset_out[b : b + per, :] = goal - (top + log2(total)) + (goal + SCALE)

    for sweep in range(1, ITERS):
        def row_sums(g, at):
            rows = weight[at, :]
            sums = []
            for i in range(GROUP):
                t = g * GROUP + i
                down = as_column(rows[i : i + 1])
                sums.append(jnp.concatenate(
                    [jnp.sum(tiles_t[t, :, lanes] * down, axis=0, keepdims=True) for lanes in cuts], axis=1))
            slot_tot[at, :] = jnp.concatenate(sums, axis=0)

        groups(row_sums)
        part_src[sweep] = functools.reduce(
            jnp.add, [jnp.where(block_of == rid[t : t + 1, :], slot_tot[t : t + 1, :], 0.0) for t in range(slots)])
        src_buf[sweep, pl.ds(my_c, 1)] = part_src[sweep][None]
        waits += send_src(sweep)
        if sweep == 1:
            dense()
        scaling = goal_a / functools.reduce(jnp.add, get_src(sweep))
        put_columns(scaling)

        def col_sums(g, at):
            sums = []
            for i in range(GROUP):
                t = g * GROUP + i
                down = columns[brows[t]]
                sums.append(jnp.concatenate(
                    [jnp.sum(tiles_s[t, :, lanes] * down, axis=0, keepdims=True) for lanes in cuts], axis=1))
            slot_tot[at, :] = jnp.concatenate(sums, axis=0)

        groups(col_sums)
        tgt_buf[sweep, 0] = anchor[...] * slot_tot[...]
        waits += send_tgt(sweep)
        if sweep == ITERS - 1:
            src_out[...] = (src_row[...] + log2(scaling)) * LN2
            if sums_out.shape[0] > n_rows * slots:
                sums_out[n_rows * slots :, :] = jnp.zeros((sums_out.shape[0] - n_rows * slots, bs), jnp.float32)
            for k in range(n_rows):
                if k:
                    tgt_copy(sweep, k).wait_recv()
                frm = split_peer(my_r, k, n_rows)[1]
                sums_out[pl.ds(pl.multiple_of(frm * slots, GROUP), slots), :] = tgt_buf[sweep, k]
            continue
        goal_b = jnp.exp2(lt_piece[...] + SCALE)
        total = jnp.zeros((slots, bs), jnp.float32)
        for k in range(n_rows):
            if k:
                tgt_copy(sweep, k).wait_recv()
            total = fold(sweep, k, jnp.add, total, 0.0)
        weight[...] = jnp.where(alive, anchor[...] * (goal_b / total), 0.0)
    for copy in waits:
        copy.wait_send()


def final_kernel(source, sums, into, offset, src_out, tgt_out):
    blocks, bs = offset.shape
    halves = bs // LANES
    pick = into[...].astype(jnp.bfloat16)
    rest = sums[...]
    total = None
    for _ in range(3):
        part = rest.astype(jnp.bfloat16)
        rest = rest - part.astype(jnp.float32)
        here = jnp.dot(pick, part, preferred_element_type=jnp.float32)
        total = here if total is None else total + here
    target = (offset[...] - log2(total)) * LN2
    for h in range(halves):
        tgt_out[pl.ds(h, blocks, stride=halves), :] = target[:, h * LANES : (h + 1) * LANES]
        src_out[pl.ds(h, source.shape[0], stride=halves), :] = source[:, h * LANES : (h + 1) * LANES]


def per_device(n_rows, n_cols, costs, block_rows, block_cols, live, log_source, log_target):
    tiles = costs[0, 0]
    slots, bs, _ = tiles.shape
    src_rows = log_source.shape[0] // LANES
    tgt_rows = log_target.shape[0] // LANES
    row_blocks = log_source.shape[0] // bs
    f32 = jnp.float32
    halves = bs // LANES
    dma = pltpu.SemaphoreType.DMA
    smem = pl.BlockSpec(memory_space=pltpu.SMEM)
    vmem = pl.BlockSpec(memory_space=pltpu.VMEM)
    found = pl.cdiv(n_rows * slots, LANES) * LANES
    blocks = log_target.shape[0] // bs
    source, sums, into, offset = pl.pallas_call(
        functools.partial(kernel, n_rows, n_cols),
        out_shape=(
            jax.ShapeDtypeStruct((row_blocks, bs), f32),
            jax.ShapeDtypeStruct((found, bs), f32),
            jax.ShapeDtypeStruct((blocks, found), f32),
            jax.ShapeDtypeStruct((blocks, bs), f32),
        ),
        in_specs=[smem, smem, smem, pl.BlockSpec(memory_space=pl.ANY), vmem, vmem],
        out_specs=(vmem, vmem, vmem, vmem),
        scratch_shapes=[
            pltpu.VMEM((slots, bs, bs), tiles.dtype),
            pltpu.VMEM((slots, bs, bs), f32),
            pltpu.VMEM((slots, bs, bs), f32),
            pltpu.VMEM((slots, bs), jnp.int32),
            pltpu.VMEM((slots, bs), jnp.int32),
            pltpu.VMEM((slots, bs), f32),
            pltpu.VMEM((slots, bs), f32),
            pltpu.VMEM((ITERS, row_blocks, bs), f32),
            pltpu.VMEM((row_blocks, bs), f32),
            pltpu.VMEM((row_blocks, bs, LANES), f32),
            pltpu.VMEM((slots, bs), f32),
            pltpu.VMEM((slots, bs), f32),
            pltpu.VMEM((slots, bs), f32),
            pltpu.VMEM((found, LANES), f32),
            pltpu.VMEM((found, bs), f32),
            pltpu.VMEM((n_rows, slots, LANES), jnp.int32),
            pltpu.VMEM((ITERS, n_cols, row_blocks, bs), f32),
            pltpu.VMEM((ITERS, n_rows, slots, bs), f32),
            dma((slots // GROUP,)),
            dma((n_rows,)), dma((n_rows,)),
            dma((ITERS, n_cols)), dma((ITERS, n_cols)),
            dma((ITERS, n_rows)), dma((ITERS, n_rows)),
        ],
        compiler_params=pltpu.CompilerParams(collective_id=0, has_side_effects=True),
    )(
        block_rows.reshape(-1), block_cols.reshape(-1), live.reshape(-1), tiles,
        log_source.reshape(src_rows, LANES), log_target.reshape(tgt_rows, LANES),
    )
    source, target = pl.pallas_call(
        final_kernel,
        out_shape=(jax.ShapeDtypeStruct((src_rows, LANES), f32), jax.ShapeDtypeStruct((tgt_rows, LANES), f32)),
        in_specs=[vmem] * 4,
        out_specs=(vmem, vmem),
    )(source, sums, into, offset)
    return source.reshape(-1), target.reshape(-1)


def solution(mesh):
    in_specs = (
        P("rows", "cols", None, None, None),
        P("rows", "cols", None),
        P("rows", "cols", None),
        P("rows", "cols"),
        P("rows"),
        P("cols"),
    )
    out_specs = (P("rows"), P("cols"))
    body = functools.partial(per_device, mesh.shape["rows"], mesh.shape["cols"])
    return jax.shard_map(body, mesh=mesh, in_specs=in_specs, out_specs=out_specs, check_vma=False)
```

```python
import functools

import jax
import jax.numpy as jnp
from jax import lax
from jax.experimental import pallas as pl
from jax.experimental.pallas import tpu as pltpu
from jax.sharding import PartitionSpec as P

ITERS = 3
NEG = -1e30
LOG2E = 1.4426950408889634
LN2 = 0.6931471805599453
LANES = 128
GROUP = 8
UNROLL = True
HEAD = 28.0
SCALE = 66.0
MESH = pl.DeviceIdType.MESH


def log2(x):
    return jnp.log(x) * LOG2E


def split_peer(me, k, n):
    if n & (n - 1):
        return lax.rem(me + k, n), lax.rem(me + n - k, n)
    other = me
    bit = 1
    while bit <= k:
        if k & bit:
            other = other + bit - 2 * bit * lax.rem(lax.div(me, bit), 2)
        bit *= 2
    return other, other


def far_first(n):
    return sorted(range(1, n), key=lambda k: (-(k // 2), k % 2))


def kernel(
    n_rows, n_cols,
    brows, bcols, live, costs, log_src, log_tgt,
    src_out, sums_out, into_out, offset_out,
    tiles, tiles_s, tiles_t, rid, cid, base, slot_tot, part_src, src_row, columns, anchor, weight, lt_piece, names, order, pick,
    cid_all, src_buf, tgt_buf,
    load_sem, cid_send, cid_recv, src_send, src_recv, tgt_send, tgt_recv,
):
    slots, bs, _ = tiles.shape
    halves = bs // LANES
    row_blocks = src_row.shape[0]
    my_r = lax.axis_index("rows")
    my_c = lax.axis_index("cols")

    barrier = pltpu.get_barrier_semaphore()
    for k in range(n_cols - 1, 0, -1):
        pl.semaphore_signal(barrier, inc=1, device_id=(my_r, split_peer(my_c, k, n_cols)[0]), device_id_type=MESH)
    for k in far_first(n_rows):
        pl.semaphore_signal(barrier, inc=1, device_id=(split_peer(my_r, k, n_rows)[0], my_c), device_id_type=MESH)

    loads = []
    for c in range(slots // GROUP):
        part = pl.ds(c * GROUP, GROUP)
        loads.append(pltpu.make_async_copy(costs.at[part], tiles.at[part], load_sem.at[c]))
        loads[-1].start()

    count = live[0]
    for t in range(slots):
        okay = t < count
        rid[t : t + 1, :] = jnp.full((1, bs), jnp.where(okay, brows[t], -1), jnp.int32)
        cid[t : t + 1, :] = jnp.full((1, bs), jnp.where(okay, bcols[t], -1), jnp.int32)
    cid_all[0] = cid[:, :LANES]

    def remote(along, k, src, dst, send_sem, recv_sem):
        if along == "rows":
            peer = (split_peer(my_r, k, n_rows)[0], my_c)
        else:
            peer = (my_r, split_peer(my_c, k, n_cols)[0])
        return pltpu.make_async_remote_copy(
            src_ref=src, dst_ref=dst, send_sem=send_sem.at[k], recv_sem=recv_sem.at[k],
            device_id=peer, device_id_type=MESH)

    def start(copies):
        for copy in copies:
            copy.start()
        return copies

    def as_column(row):
        return jnp.concatenate(
            [jnp.broadcast_to(row[:, h * LANES : (h + 1) * LANES], (LANES, LANES)).T for h in range(halves)], axis=0)

    def turned_parts(values):
        parts, rest = [], values
        for _ in range(3):
            part = rest.astype(jnp.bfloat16).astype(jnp.float32)
            rest = rest - part
            parts.append(part)
            if slots > values.shape[0]:
                parts.append(jnp.zeros((slots - values.shape[0], bs), jnp.float32))
        parts.append(jnp.zeros((LANES - 3 * slots, bs), jnp.float32))
        stack = jnp.concatenate(parts, axis=0)
        return jnp.concatenate([stack[:, lanes].T for lanes in cuts], axis=0).astype(jnp.bfloat16)

    def spread(turned, t):
        return lax.dot_general(turned, pick[t], (((1,), (0,)), ((), ())), preferred_element_type=jnp.float32)

    def groups(body):
        def step(g, _):
            body(g, pl.ds(pl.multiple_of(g * GROUP, GROUP), GROUP))
            return 0

        lax.fori_loop(0, slots // GROUP, step, 0, unroll=UNROLL)

    cuts = [slice(h * LANES, (h + 1) * LANES) for h in range(halves)]
    eye = (lax.broadcasted_iota(jnp.int32, (bs, bs), 0) == lax.broadcasted_iota(jnp.int32, (bs, bs), 1))
    eye = eye.astype(jnp.float32).astype(jnp.bfloat16)
    for c in range(slots // GROUP):
        loads[c].wait()

        at = slice(c * GROUP, (c + 1) * GROUP)
        for lanes in cuts:
            lows, tots = [], []
            for t in range(c * GROUP, (c + 1) * GROUP):
                turned = lax.dot_general(
                    eye, tiles[t, lanes, :], (((1,), (1,)), ((), ())), preferred_element_type=jnp.float32)
                cost = turned * LOG2E
                tiles_t[t, :, lanes] = cost
                low = jnp.min(cost, axis=0, keepdims=True)
                lows.append(low)
                tots.append(jnp.sum(jnp.exp2(low - cost), axis=0, keepdims=True))
            base[at, lanes] = -jnp.concatenate(lows, axis=0)
            slot_tot[at, lanes] = jnp.concatenate(tots, axis=0)

    block_of = lax.broadcasted_iota(jnp.int32, (row_blocks, bs), 0)
    found = base[...] + log2(slot_tot[...])
    masked = [jnp.where(block_of == rid[t : t + 1, :], found[t : t + 1, :], NEG) for t in range(slots)]
    top = functools.reduce(jnp.maximum, masked)
    total = functools.reduce(jnp.add, [jnp.exp2(value - top) for value in masked])
    part_src[0] = top + log2(total)
    src_buf[0, pl.ds(my_c, 1)] = part_src[0][None]

    pl.semaphore_wait(barrier, n_rows + n_cols - 2)

    def send_src(sweep):
        return start([
            remote("cols", k, part_src.at[sweep], src_buf.at[sweep, my_c], src_send.at[sweep], src_recv.at[sweep])
            for k in range(n_cols - 1, 0, -1)])

    def get_src(sweep):
        for k in range(1, n_cols):
            frm = split_peer(my_c, k, n_cols)[1]
            remote("cols", k, part_src.at[sweep], src_buf.at[sweep, frm], src_send.at[sweep], src_recv.at[sweep]).wait_recv()
        return [src_buf[sweep, k] for k in range(n_cols)]

    def tgt_copy(sweep, k):
        return remote("rows", k, tgt_buf.at[sweep, 0], tgt_buf.at[sweep, k], tgt_send.at[sweep], tgt_recv.at[sweep])

    def send_tgt(sweep):
        return start([tgt_copy(sweep, k) for k in far_first(n_rows)])

    def cid_copy(k):
        return remote("rows", k, cid_all.at[0], cid_all.at[k], cid_send, cid_recv)

    waits = send_src(0)
    waits += start([cid_copy(k) for k in far_first(n_rows)])

    line = lax.rem(lax.broadcasted_iota(jnp.int32, (LANES, LANES), 0), slots)
    inside = lax.broadcasted_iota(jnp.int32, (LANES, LANES), 0) < 3 * slots

    def natural(g, at):
        for i in range(GROUP):
            here = jnp.where(inside & (line == g * GROUP + i), 1.0, 0.0)
            pick[g * GROUP + i] = here.astype(jnp.bfloat16)
            tiles_s[g * GROUP + i] = tiles[g * GROUP + i].astype(jnp.float32) * LOG2E

    groups(natural)

    for t in range(slots):
        col_at = bcols[t] * halves
        for h, lanes in enumerate(cuts):
            lt_piece[t : t + 1, lanes] = log_tgt[pl.ds(col_at + h, 1), :] * LOG2E
    log_a = jnp.concatenate([log_src[pl.ds(h, row_blocks, stride=halves), :] for h in range(halves)], axis=1) * LOG2E

    theirs = get_src(0)
    top = functools.reduce(jnp.maximum, theirs)
    total = functools.reduce(jnp.add, [jnp.exp2(value - top) for value in theirs])
    first = log_a - (top + log2(total))
    src_row[...] = first

    def put_columns(values):
        turned = turned_parts(values)
        for b in range(row_blocks):
            columns[b] = spread(turned, b) if b % 2 else as_column(values[b : b + 1, :])

    put_columns(first)

    def first_col(g, at):
        for lanes in cuts:
            tops, tots = [], []
            for i in range(GROUP):
                t = g * GROUP + i
                score = columns[brows[t]] - tiles_s[t, :, lanes]
                top = jnp.max(score, axis=0, keepdims=True) - HEAD
                entry = jnp.exp2(score - top)
                tiles_s[t, :, lanes] = entry
                tops.append(top)
                tots.append(jnp.sum(entry, axis=0, keepdims=True))
            base[at, lanes] = jnp.concatenate(tops, axis=0)
            slot_tot[at, lanes] = jnp.concatenate(tots, axis=0)

    groups(first_col)
    alive = cid[...] >= 0
    tgt_buf[0, 0] = jnp.where(alive, base[...] + log2(slot_tot[...]), NEG)
    waits += send_tgt(0)

    def first_turned(g, at):
        bases = base[at, :]
        for i in range(GROUP):
            t = g * GROUP + i
            down = as_column(bases[i : i + 1])
            row = src_row[pl.ds(brows[t], 1), :]
            for lanes in cuts:
                tiles_t[t, :, lanes] = jnp.exp2((row[:, lanes] - tiles_t[t, :, lanes]) - down)

    groups(first_turned)
    for k in range(1, n_rows):
        cid_copy(k).wait_recv()

    def wide(mask):
        return jnp.concatenate([mask] * halves, axis=1)

    def fold(sweep, k, op, so_far, fill):
        ids = cid[:, :LANES]

        def body(g, so_far):
            at = pl.ds(pl.multiple_of(g * GROUP, GROUP), GROUP)
            theirs, values = cid_all[k, at, :], tgt_buf[sweep, k, at, :]
            for i in range(GROUP):
                so_far = op(so_far, jnp.where(wide(ids == theirs[i : i + 1]), values[i : i + 1], fill))
            return so_far

        return lax.fori_loop(0, slots // GROUP, body, so_far, unroll=n_rows <= 4)

    top = jnp.full((slots, bs), NEG, jnp.float32)
    for k in range(n_rows):
        if k:
            tgt_copy(0, k).wait_recv()
        top = fold(0, k, jnp.maximum, top, NEG)
    total = jnp.zeros((slots, bs), jnp.float32)
    for k in range(n_rows):
        total = fold(0, k, lambda so_far, value: so_far + jnp.exp2(value - top), total, NEG)
    gain = lt_piece[...] - (top + log2(total)) + (base[...] + SCALE)
    anchor[...] = jnp.where(alive, jnp.exp2(gain), 0.0)
    weight[...] = anchor[...]
    goal_a = jnp.exp2(log_a + SCALE)

    def dense():
        blocks = offset_out.shape[0]
        padded = sums_out.shape[0]
        if padded > n_rows * slots:
            names[n_rows * slots :, :] = jnp.full((padded - n_rows * slots, LANES), -2.0, jnp.float32)
        for k in range(n_rows):
            frm = split_peer(my_r, k, n_rows)[1]
            names[pl.ds(pl.multiple_of(frm * slots, GROUP), slots), :] = cid_all[k].astype(jnp.float32)
            order[pl.ds(pl.multiple_of(frm * slots, GROUP), slots), :] = tgt_buf[0, k]
        for j in range(padded // LANES):
            line = names[j * LANES : (j + 1) * LANES, :].T[0:1, :]
            into_out[:, j * LANES : (j + 1) * LANES] = jnp.where(
                line == lax.broadcasted_iota(jnp.int32, (blocks, LANES), 0).astype(jnp.float32), 1.0, 0.0)
        per = 16 if blocks % 16 == 0 else blocks
        for b in range(0, blocks, per):
            block = (lax.broadcasted_iota(jnp.int32, (per, LANES), 0) + b).astype(jnp.float32)

            def walk(op, start):
                def body(g, so_far):
                    at = pl.ds(pl.multiple_of(g * GROUP, GROUP), GROUP)
                    theirs, values = names[at, :], order[at, :]
                    for i in range(GROUP):
                        so_far = op(so_far, jnp.where(wide(block == theirs[i : i + 1]), values[i : i + 1], NEG))
                    return so_far

                return lax.fori_loop(0, n_rows * slots // GROUP, body, start)

            top = walk(jnp.maximum, jnp.full((per, bs), NEG, jnp.float32))
            total = walk(lambda so_far, value: so_far + jnp.exp2(value - top), jnp.zeros((per, bs), jnp.float32))
            goal = jnp.concatenate(
                [log_tgt[pl.ds(b * halves + h, per, stride=halves), :] for h in range(halves)], axis=1) * LOG2E
            offset_out[b : b + per, :] = goal - (top + log2(total)) + (goal + SCALE)

    for sweep in range(1, ITERS):
        turned = turned_parts(weight[...])

        def row_sums(g, at):
            rows = weight[at, :]
            sums = []
            for i in range(GROUP):
                t = g * GROUP + i
                down = spread(turned, t) if i % 2 else as_column(rows[i : i + 1])
                sums.append(jnp.concatenate(
                    [jnp.sum(tiles_t[t, :, lanes] * down, axis=0, keepdims=True) for lanes in cuts], axis=1))
            slot_tot[at, :] = jnp.concatenate(sums, axis=0)

        groups(row_sums)
        part_src[sweep] = functools.reduce(
            jnp.add, [jnp.where(block_of == rid[t : t + 1, :], slot_tot[t : t + 1, :], 0.0) for t in range(slots)])
        src_buf[sweep, pl.ds(my_c, 1)] = part_src[sweep][None]
        waits += send_src(sweep)
        if sweep == 1:
            dense()
        scaling = goal_a / functools.reduce(jnp.add, get_src(sweep))
        put_columns(scaling)

        def col_sums(g, at):
            sums = []
            for i in range(GROUP):
                t = g * GROUP + i
                down = columns[brows[t]]
                sums.append(jnp.concatenate(
                    [jnp.sum(tiles_s[t, :, lanes] * down, axis=0, keepdims=True) for lanes in cuts], axis=1))
            slot_tot[at, :] = jnp.concatenate(sums, axis=0)

        groups(col_sums)
        tgt_buf[sweep, 0] = anchor[...] * slot_tot[...]
        waits += send_tgt(sweep)
        if sweep == ITERS - 1:
            src_out[...] = (src_row[...] + log2(scaling)) * LN2
            if sums_out.shape[0] > n_rows * slots:
                sums_out[n_rows * slots :, :] = jnp.zeros((sums_out.shape[0] - n_rows * slots, bs), jnp.float32)
            for k in range(n_rows):
                if k:
                    tgt_copy(sweep, k).wait_recv()
                frm = split_peer(my_r, k, n_rows)[1]
                sums_out[pl.ds(pl.multiple_of(frm * slots, GROUP), slots), :] = tgt_buf[sweep, k]
            continue
        goal_b = jnp.exp2(lt_piece[...] + SCALE)
        total = jnp.zeros((slots, bs), jnp.float32)
        for k in range(n_rows):
            if k:
                tgt_copy(sweep, k).wait_recv()
            total = fold(sweep, k, jnp.add, total, 0.0)
        weight[...] = jnp.where(alive, anchor[...] * (goal_b / total), 0.0)
    for copy in waits:
        copy.wait_send()


def final_kernel(source, sums, into, offset, src_out, tgt_out):
    blocks, bs = offset.shape
    halves = bs // LANES
    pick = into[...].astype(jnp.bfloat16)
    rest = sums[...]
    total = None
    for _ in range(3):
        part = rest.astype(jnp.bfloat16)
        rest = rest - part.astype(jnp.float32)
        here = jnp.dot(pick, part, preferred_element_type=jnp.float32)
        total = here if total is None else total + here
    target = (offset[...] - log2(total)) * LN2
    for h in range(halves):
        tgt_out[pl.ds(h, blocks, stride=halves), :] = target[:, h * LANES : (h + 1) * LANES]
        src_out[pl.ds(h, source.shape[0], stride=halves), :] = source[:, h * LANES : (h + 1) * LANES]


def per_device(n_rows, n_cols, costs, block_rows, block_cols, live, log_source, log_target):
    tiles = costs[0, 0]
    slots, bs, _ = tiles.shape
    src_rows = log_source.shape[0] // LANES
    tgt_rows = log_target.shape[0] // LANES
    row_blocks = log_source.shape[0] // bs
    f32 = jnp.float32
    halves = bs // LANES
    dma = pltpu.SemaphoreType.DMA
    smem = pl.BlockSpec(memory_space=pltpu.SMEM)
    vmem = pl.BlockSpec(memory_space=pltpu.VMEM)
    found = pl.cdiv(n_rows * slots, LANES) * LANES
    blocks = log_target.shape[0] // bs
    source, sums, into, offset = pl.pallas_call(
        functools.partial(kernel, n_rows, n_cols),
        out_shape=(
            jax.ShapeDtypeStruct((row_blocks, bs), f32),
            jax.ShapeDtypeStruct((found, bs), f32),
            jax.ShapeDtypeStruct((blocks, found), f32),
            jax.ShapeDtypeStruct((blocks, bs), f32),
        ),
        in_specs=[smem, smem, smem, pl.BlockSpec(memory_space=pl.ANY), vmem, vmem],
        out_specs=(vmem, vmem, vmem, vmem),
        scratch_shapes=[
            pltpu.VMEM((slots, bs, bs), tiles.dtype),
            pltpu.VMEM((slots, bs, bs), f32),
            pltpu.VMEM((slots, bs, bs), f32),
            pltpu.VMEM((slots, bs), jnp.int32),
            pltpu.VMEM((slots, bs), jnp.int32),
            pltpu.VMEM((slots, bs), f32),
            pltpu.VMEM((slots, bs), f32),
            pltpu.VMEM((ITERS, row_blocks, bs), f32),
            pltpu.VMEM((row_blocks, bs), f32),
            pltpu.VMEM((row_blocks, bs, LANES), f32),
            pltpu.VMEM((slots, bs), f32),
            pltpu.VMEM((slots, bs), f32),
            pltpu.VMEM((slots, bs), f32),
            pltpu.VMEM((found, LANES), f32),
            pltpu.VMEM((found, bs), f32),
            pltpu.VMEM((slots, LANES, LANES), jnp.bfloat16),
            pltpu.VMEM((n_rows, slots, LANES), jnp.int32),
            pltpu.VMEM((ITERS, n_cols, row_blocks, bs), f32),
            pltpu.VMEM((ITERS, n_rows, slots, bs), f32),
            dma((slots // GROUP,)),
            dma((n_rows,)), dma((n_rows,)),
            dma((ITERS, n_cols)), dma((ITERS, n_cols)),
            dma((ITERS, n_rows)), dma((ITERS, n_rows)),
        ],
        compiler_params=pltpu.CompilerParams(collective_id=0, has_side_effects=True),
    )(
        block_rows.reshape(-1), block_cols.reshape(-1), live.reshape(-1), tiles,
        log_source.reshape(src_rows, LANES), log_target.reshape(tgt_rows, LANES),
    )
    source, target = pl.pallas_call(
        final_kernel,
        out_shape=(jax.ShapeDtypeStruct((src_rows, LANES), f32), jax.ShapeDtypeStruct((tgt_rows, LANES), f32)),
        in_specs=[vmem] * 4,
        out_specs=(vmem, vmem),
    )(source, sums, into, offset)
    return source.reshape(-1), target.reshape(-1)


def solution(mesh):
    in_specs = (
        P("rows", "cols", None, None, None),
        P("rows", "cols", None),
        P("rows", "cols", None),
        P("rows", "cols"),
        P("rows"),
        P("cols"),
    )
    out_specs = (P("rows"), P("cols"))
    body = functools.partial(per_device, mesh.shape["rows"], mesh.shape["cols"])
    return jax.shard_map(body, mesh=mesh, in_specs=in_specs, out_specs=out_specs, check_vma=False)
```
